32 devices in a mesh: replica: 4 (over y, core), fsdp: 4 (over z), tensor: 2 (over x).
Axes of the slice: x: 2, y: 2, z: 4, core: 2. Of those that a mesh axis runs over, the one named last changes fastest.
Arguments:
- tokens: bfloat16 [8192, 8192], P(('replica', 'fsdp')), may hold values from -6 to 6
- norm_gain: float32 [8192], replicated, may hold values from 0.1 to 1.9
- outer_base: float32 [2, 8192, 1024], P(None, 'fsdp', 'tensor'), may hold values from -0.0625 to 0.0625
- momentum: float32 [2, 8192, 1024], P(None, 'fsdp', 'tensor'), may hold values from -0.06 to 0.06
- inner_params: bfloat16 [4, 2, 8192, 1024], P('replica', None, 'fsdp', 'tensor'), may hold values from -0.0625 to 0.0625
Outputs:
- new_base: float32 [2, 8192, 1024], P(None, ('fsdp', 'replica'), 'tensor')
- new_momentum: float32 [2, 8192, 1024], P(None, ('fsdp', 'replica'), 'tensor')
- keys: bfloat16 [8192, 1024], P(('replica', 'fsdp'), 'tensor')
- values: bfloat16 [8192, 1024], P(('replica', 'fsdp'), 'tensor')
The draws below stay inside these ranges and needn't reach their ends.
All inputs are finite; a program needn't handle non-finite values.
Results may differ from the reference program's by a relative error of at most 0.018.
Values may be sent and summed in bfloat16 or wider, within the bound.
A program may use at most 128 MiB of HBM per device.

```python
import jax
import jax.numpy as jnp
from jax import lax

D = 8192
KV = 1024
TOKENS = 8192
N_REPLICA = 4


def levels(own_key, shape, split, smallest, top_value):
    level = 1.0
    for dim, blocks in split:
        heights = jax.random.uniform(jax.random.fold_in(jax.random.fold_in(own_key, 6), dim), (blocks,), jnp.float32, smallest / len(split), top_value / len(split))
        level = level * jnp.repeat(jnp.exp(heights), shape[dim] // blocks).reshape((-1,) + (1,) * (len(shape) - 1 - dim))
    return level


def normal_values(stream_key, extent, width, bound, cuts=(), kind=jnp.bfloat16):
    array = jax.random.normal(stream_key, extent, jnp.float32) * width
    if len(cuts) > 0:
        array = levels(stream_key, extent, cuts, -0.22, 0.18) * array
    return jnp.clip(array, min=-bound, max=bound).astype(kind)


def setup_inputs(seed: int = 0) -> dict:
    streams_of = jax.random.split(jax.random.key(seed), 6)
    tokens = normal_values(streams_of[0], (TOKENS, D), 1.0, 6.0, ((0, 16),))
    norm_gain = jnp.clip(1.0 + 0.18 * jax.random.normal(streams_of[1], (D,), jnp.float32), 0.1, 1.9)
    outer_base = normal_values(streams_of[2], (2, D, KV), D ** -0.5, 0.0625, ((1, 4), (2, 2)), jnp.float32)
    momentum = normal_values(streams_of[3], (2, D, KV), 0.01, 0.06, ((1, 4), (2, 2)), jnp.float32)
    inner_params = normal_values(streams_of[4], (N_REPLICA, 2, D, KV), D ** -0.5, 0.0625, ((0, 4), (2, 4), (3, 2)))
    return dict(tokens=tokens, norm_gain=norm_gain, outer_base=outer_base, momentum=momentum, inner_params=inner_params)


momentum_rate = 0.9
outer_rate = 0.7
epsilon = 1e-05

def reference(tokens, norm_gain, outer_base, momentum, inner_params):
    deltas = (outer_base[None] - inner_params.astype(jnp.float32)).astype(jnp.bfloat16)
    average = lax.optimization_barrier(jnp.sum(deltas.astype(jnp.float32), axis=0)) / N_REPLICA
    new_momentum = momentum_rate * momentum + average
    new_base = outer_base - outer_rate * (average + momentum_rate * new_momentum)
    weights = new_base.astype(jnp.bfloat16)
    inputs = tokens.astype(jnp.float32)
    scale = lax.rsqrt(lax.optimization_barrier(jnp.mean(inputs * inputs, axis=-1, keepdims=True)) + epsilon)
    normed = (inputs * scale * norm_gain).astype(jnp.bfloat16)
    keys = jnp.dot(normed, weights[0], preferred_element_type=jnp.float32).astype(jnp.bfloat16)
    values = jnp.dot(normed, weights[1], preferred_element_type=jnp.float32).astype(jnp.bfloat16)
    return (new_base, new_momentum, keys, values)
```

```python
import functools

import jax
import jax.numpy as jnp
from jax import lax
from jax.experimental import pallas as pl
from jax.experimental.pallas import tpu as pltpu
from jax.sharding import PartitionSpec as P

momentum_rate = 0.9
outer_rate = 0.7
epsilon = 1e-05
MESH = pl.DeviceIdType.MESH
CHUNKS = 4
FIRST_Z = 3


def kernel(
    depth, tok_h, gain_ref, base_h, mom_h, inner_h,
    nb_h, nm_h, keys_ref, values_ref,
    tok, base, inner, mom, nb, w, ps, pr, ys, yr, acc,
    in_sem, tok_sem, out_sem, ps_sem, pr_sem, ys_sem, yr_sem,
    w_recv, right_sem, left_sem, cross_sem, pair_sem,
):
    r = lax.axis_index("replica")
    z = lax.axis_index("fsdp")
    x = lax.axis_index("tensor")
    y, c = r // 2, r % 2
    oy, oc = 1 - y, 1 - c
    pair = (y * 2 + oc, z, x)
    cross = (oy * 2 + c, z, x)
    right = (r, z + 1, x)
    left = (r, z - 1, x)
    rows = w.shape[-2]
    token_rows = tok.shape[0]

    def load(k):
        m, h = k // 2, k % 2
        return (
            pltpu.make_async_copy(base_h.at[m, :, h], base.at[k], in_sem.at[k, 0]),
            pltpu.make_async_copy(inner_h.at[m, :, h], inner.at[k], in_sem.at[k, 1]),
        )

    def load_momentum(k):
        return pltpu.make_async_copy(mom_h.at[k // 2, r, k % 2], mom.at[k], in_sem.at[k, 2])

    load_tokens = pltpu.make_async_copy(tok_h, tok, tok_sem)
    for k in range(CHUNKS):
        for copy in load(k):
            copy.start()
    load_tokens.start()
    for k in range(CHUNKS):
        load_momentum(k).start()
    acc[...] = jnp.zeros_like(acc)

    barrier = pltpu.get_barrier_semaphore()
    for peer in (pair, cross):
        pl.semaphore_signal(barrier, inc=1, device_id=peer, device_id_type=MESH)

    @pl.when(z < depth - 1)
    def _():
        pl.semaphore_signal(barrier, inc=1, device_id=right, device_id_type=MESH)

    @pl.when(z > 0)
    def _():
        pl.semaphore_signal(barrier, inc=1, device_id=left, device_id_type=MESH)

    neighbours = jnp.where(z < depth - 1, 1, 0) + jnp.where(z > 0, 1, 0)
    pl.semaphore_wait(barrier, 2 + neighbours)

    def delta(k, target):
        return (base[k, target] - inner[k, target].astype(jnp.float32)).astype(jnp.bfloat16)

    def to_pair(k):
        return pltpu.make_async_remote_copy(
            ps.at[k], pr.at[k], ps_sem.at[k], pr_sem.at[k], device_id=pair, device_id_type=MESH)

    def to_cross(k):
        return pltpu.make_async_remote_copy(
            ys.at[k], yr.at[k], ys_sem.at[k], yr_sem.at[k], device_id=cross, device_id_type=MESH)

    for k in range(CHUNKS + 1):
        if k < CHUNKS:
            for copy in load(k):
                copy.wait()
            ps[k, 1] = delta(k, oy * 2 + oc)
            ps[k, 0] = delta(k, y * 2 + oc)
            to_pair(k).start()
        if k > 0:
            j = k - 1
            to_pair(j).wait_recv()
            ys[j] = (delta(j, oy * 2 + c).astype(jnp.float32) + pr[j, 1].astype(jnp.float32)).astype(jnp.bfloat16)
            to_cross(j).start()

    def send(yl, o, k, peer, sem):
        block = w.at[c, yl, o, k]
        return pltpu.make_async_remote_copy(
            block, block, sem, w_recv.at[c, yl, o, k], device_id=peer, device_id_type=MESH)

    def send_right(yl, o, k):
        return send(yl, o, k, right, right_sem.at[yl, o, k])

    def send_left(yl, o, k):
        return send(yl, o, k, left, left_sem.at[yl, o, k])

    def send_cross(yl, o, k):
        return send(yl, o, k, cross, cross_sem.at[o, k])

    def send_pair(yl, o, k):
        return send(yl, o, k, pair, pair_sem.at[yl, o, k])

    def arrived(cc, yl, o, k):
        block = w.at[cc, yl, o, k]
        pltpu.make_async_copy(block, block, w_recv.at[cc, yl, o, k]).wait()

    def along(yl, o, k, do_right, do_left):
        if do_right:
            @pl.when(z < depth - 1)
            def _():
                send_right(yl, o, k).start()
        if do_left:
            @pl.when(z > 0)
            def _():
                send_left(yl, o, k).start()

    def multiply(cc, yl, o, k):
        m, h = k // 2, k % 2
        first = pl.multiple_of(((o * 4 + yl * 2 + cc) * 2 + h) * rows, rows)
        acc[m] += jnp.dot(tok[:, pl.ds(first, rows)], w[cc, yl, o, k], preferred_element_type=jnp.float32)

    def normalize(i):
        at = pl.ds(pl.multiple_of(i * 16, 16), 16)
        value = tok[at, :].astype(jnp.float32)
        scale = lax.rsqrt(jnp.mean(value * value, axis=-1, keepdims=True) + epsilon)
        tok[at, :] = (value * scale * gain_ref[...]).astype(jnp.bfloat16)

    def out_copies(k):
        m, h = k // 2, k % 2
        return (
            pltpu.make_async_copy(nb.at[k], nb_h.at[m, h], out_sem.at[k, 0]),
            pltpu.make_async_copy(mom.at[k], nm_h.at[m, h], out_sem.at[k, 1]),
        )

    load_tokens.wait()
    strips = token_rows // 16
    for k in range(CHUNKS):
        lax.fori_loop(k * strips // CHUNKS, (k + 1) * strips // CHUNKS, lambda i, s: (normalize(i), s)[1], 0)
        load_momentum(k).wait()
        to_cross(k).wait_recv()
        total = (
            delta(k, r).astype(jnp.float32) + pr[k, 0].astype(jnp.float32) + yr[k].astype(jnp.float32))
        average = total / 4
        new_momentum = momentum_rate * mom[k] + average
        new_base = base[k, r] - outer_rate * (average + momentum_rate * new_momentum)
        w[c, y, z, k] = new_base.astype(jnp.bfloat16)
        mom[k] = new_momentum
        nb[k] = new_base
        along(y, z, k, True, True)
        send_cross(y, z, k).start()
        send_pair(y, z, k).start()
        for copy in out_copies(k):
            copy.start()

    def loop(count, body):
        lax.fori_loop(0, count, lambda i, s: (body(i), s)[1], 0)

    def both_sides(g, body):
        @pl.when(z - g >= 0)
        def _():
            body(z - g, True, False)

        @pl.when(z + g < depth)
        def _():
            body(z + g, False, True)

    def multiply_all(g, blocks, place):
        def one(i):
            cc, side, b = (i // 2) % 2, i % 2, i // 4
            o = z + (2 * side - 1) * g
            yl, k = place(b)

            @pl.when((o >= 0) & (o < depth))
            def _():
                @pl.when(cc == 1)
                def _():
                    arrived(oc, yl, o, k)
                multiply((c + cc) % 2, yl, o, k)
        loop(4 * blocks, one)

    def own_products(i):
        k, cc = i // 2, i % 2

        @pl.when(cc == 1)
        def _():
            arrived(oc, y, z, k)
        multiply((c + cc) % 2, y, z, k)

    loop(2 * CHUNKS, own_products)

    late = CHUNKS - FIRST_Z

    def first_stage(g):
        def one(k):
            def relay(o, do_right, do_left):
                arrived(c, y, o, k)
                along(y, o, k, do_right, do_left)
                send_cross(y, o, k).start()
                send_pair(y, o, k).start()
            both_sides(g, relay)
        loop(FIRST_Z, one)

        @pl.when(g == min(2, depth - 1))
        def _():
            for k in range(FIRST_Z, CHUNKS):
                arrived(c, oy, z, k)
                along(oy, z, k, True, True)
                send_pair(oy, z, k).start()

        multiply_all(g, FIRST_Z, lambda b: (y, b))

    lax.fori_loop(1, depth, lambda g, s: (first_stage(g), s)[1], 0)

    def from_cross(k):
        arrived(c, oy, z, k)
        send_pair(oy, z, k).start()

    loop(FIRST_Z, from_cross)

    def cross_products(i):
        k, cc = i // 2, i % 2

        @pl.when(cc == 1)
        def _():
            arrived(oc, oy, z, k)
        multiply((c + cc) % 2, oy, z, k)

    loop(2 * CHUNKS, cross_products)

    def second_stage(g):
        def one(i):
            yl, k = i % 2, FIRST_Z + i // 2

            def relay(o, do_right, do_left):
                arrived(c, yl, o, k)
                along(yl, o, k, do_right, do_left)
                send_pair(yl, o, k).start()
            both_sides(g, relay)
        loop(2 * late, one)
        multiply_all(g, 2 * late, lambda b: (b % 2, FIRST_Z + b // 2))

        def two(k):
            def relay(o, do_right, do_left):
                arrived(c, oy, o, k)
                send_pair(oy, o, k).start()
            both_sides(g, relay)
        loop(FIRST_Z, two)
        multiply_all(g, FIRST_Z, lambda b: (oy, b))

    lax.fori_loop(1, depth, lambda g, s: (second_stage(g), s)[1], 0)

    keys_ref[...] = acc[0].astype(keys_ref.dtype)
    values_ref[...] = acc[1].astype(values_ref.dtype)

    for k in range(CHUNKS):
        to_pair(k).wait_send()
        to_cross(k).wait_send()
        for copy in out_copies(k):
            copy.wait()

    def drain(i):
        o, k = i // CHUNKS, i % CHUNKS

        @pl.when((k < FIRST_Z) | (o == z))
        def _():
            send_cross(y, o, k).wait_send()

        for yl in range(2):
            send_pair(yl, o, k).wait_send()

            @pl.when((k >= FIRST_Z) | (yl == y))
            def _():
                @pl.when((o <= z) & (z < depth - 1))
                def _():
                    send_right(yl, o, k).wait_send()

                @pl.when((o >= z) & (z > 0))
                def _():
                    send_left(yl, o, k).wait_send()

    loop(depth * CHUNKS, drain)


def on_device(tokens, norm_gain, outer_base, momentum, inner_params):
    depth = lax.axis_size("fsdp")
    replicas = lax.axis_size("replica")
    assert replicas == 4
    quarter = outer_base.shape[1] // replicas
    rows, columns = quarter // 2, outer_base.shape[2]
    count, features = tokens.shape
    split = (2, replicas, 2, rows, columns)
    anywhere = pl.BlockSpec(memory_space=pl.ANY)
    vmem = pl.BlockSpec(memory_space=pltpu.VMEM)
    dma = pltpu.SemaphoreType.DMA
    f32, bf16 = jnp.float32, jnp.bfloat16
    piece = (rows, columns)
    new_base, new_momentum, keys, values = pl.pallas_call(
        functools.partial(kernel, depth),
        name="outer_step",
        out_shape=(
            jax.ShapeDtypeStruct((2, 2) + piece, f32),
            jax.ShapeDtypeStruct((2, 2) + piece, f32),
            jax.ShapeDtypeStruct((count, columns), bf16),
            jax.ShapeDtypeStruct((count, columns), bf16),
        ),
        in_specs=[anywhere, vmem, anywhere, anywhere, anywhere],
        out_specs=(anywhere, anywhere, vmem, vmem),
        scratch_shapes=[
            pltpu.VMEM((count, features), bf16),
            pltpu.VMEM((CHUNKS, replicas) + piece, f32),
            pltpu.VMEM((CHUNKS, replicas) + piece, bf16),
            pltpu.VMEM((CHUNKS,) + piece, f32),
            pltpu.VMEM((CHUNKS,) + piece, f32),
            pltpu.VMEM((2, 2, depth, CHUNKS) + piece, bf16),
            pltpu.VMEM((CHUNKS, 2) + piece, bf16),
            pltpu.VMEM((CHUNKS, 2) + piece, bf16),
            pltpu.VMEM((CHUNKS,) + piece, bf16),
            pltpu.VMEM((CHUNKS,) + piece, bf16),
            pltpu.VMEM((2, count, columns), f32),
            dma((CHUNKS, 3)), dma, dma((CHUNKS, 2)),
            dma((CHUNKS,)), dma((CHUNKS,)), dma((CHUNKS,)), dma((CHUNKS,)),
            dma((2, 2, depth, CHUNKS)),
            dma((2, depth, CHUNKS)), dma((2, depth, CHUNKS)), dma((depth, CHUNKS)), dma((2, depth, CHUNKS)),
        ],
        compiler_params=pltpu.CompilerParams(
            collective_id=0, has_side_effects=True, vmem_limit_bytes=60 * 1024 * 1024),
    )(
        tokens,
        norm_gain.reshape(1, features),
        outer_base.reshape(split),
        momentum.reshape(split),
        inner_params.reshape(split),
    )
    share = (2, quarter, columns)
    return new_base.reshape(share), new_momentum.reshape(share), keys, values


def solution(mesh):
    placed = (
        P(("replica", "fsdp"), None),
        P(),
        P(None, "fsdp", "tensor"),
        P(None, "fsdp", "tensor"),
        P("replica", None, "fsdp", "tensor"),
    )
    return jax.shard_map(
        on_device,
        mesh=mesh,
        in_specs=placed,
        out_specs=(
            P(None, ("fsdp", "replica"), "tensor"),
            P(None, ("fsdp", "replica"), "tensor"),
            P(("replica", "fsdp"), "tensor"),
            P(("replica", "fsdp"), "tensor"),
        ),
        check_vma=False,
    )
```

```python
import functools

import jax
import jax.numpy as jnp
from jax import lax
from jax.experimental import pallas as pl
from jax.experimental.pallas import tpu as pltpu
from jax.sharding import PartitionSpec as P

momentum_rate = 0.9
outer_rate = 0.7
epsilon = 1e-05
MESH = pl.DeviceIdType.MESH
HALVES = 2
WIDTH = 256


def kernel(
    depth, chunks, tok_h, gain_ref, base_h, mom_h, inner_h,
    nb_h, nm_h, keys_ref, values_ref,
    tok, base, inner, mom, nb, w, ps, pr, ys, yr, acc,
    in_sem, tok_sem, out_sem, ps_sem, pr_sem, ys_sem, yr_sem,
    w_recv, right_sem, left_sem, cross_sem, pair_sem,
):
    r = lax.axis_index("replica")
    z = lax.axis_index("fsdp")
    x = lax.axis_index("tensor")
    y, c = r // 2, r % 2
    oy, oc = 1 - y, 1 - c
    pair = (y * 2 + oc, z, x)
    cross = (oy * 2 + c, z, x)
    right = (r, z + 1, x)
    left = (r, z - 1, x)
    rows, width = w.shape[-2:]
    token_rows = tok.shape[0]
    strips_across = chunks // (2 * HALVES)
    first_z = 3 * chunks // 4

    def part(k):
        return k // (HALVES * strips_across), (k // strips_across) % HALVES, k % strips_across

    def strip(v):
        return pl.ds(v * width, width)

    def load(k):
        m, h, v = part(k)
        return (
            pltpu.make_async_copy(base_h.at[m, :, h, :, strip(v)], base.at[k], in_sem.at[k, 0]),
            pltpu.make_async_copy(inner_h.at[m, :, h, :, strip(v)], inner.at[k], in_sem.at[k, 1]),
        )

    def load_momentum(k):
        m, h, v = part(k)
        return pltpu.make_async_copy(mom_h.at[m, r, h, :, strip(v)], mom.at[k], in_sem.at[k, 2])

    load_tokens = pltpu.make_async_copy(tok_h, tok, tok_sem)
    for k in range(chunks):
        for copy in load(k):
            copy.start()
    load_tokens.start()
    for k in range(chunks):
        load_momentum(k).start()
    acc[...] = jnp.zeros_like(acc)

    barrier = pltpu.get_barrier_semaphore()
    for peer in (pair, cross):
        pl.semaphore_signal(barrier, inc=1, device_id=peer, device_id_type=MESH)

    @pl.when(z < depth - 1)
    def _():
        pl.semaphore_signal(barrier, inc=1, device_id=right, device_id_type=MESH)

    @pl.when(z > 0)
    def _():
        pl.semaphore_signal(barrier, inc=1, device_id=left, device_id_type=MESH)

    neighbours = jnp.where(z < depth - 1, 1, 0) + jnp.where(z > 0, 1, 0)
    pl.semaphore_wait(barrier, 2 + neighbours)

    def delta(k, target):
        return (base[k, target] - inner[k, target].astype(jnp.float32)).astype(jnp.bfloat16)

    def to_pair(k):
        return pltpu.make_async_remote_copy(
            ps.at[k], pr.at[k], ps_sem.at[k], pr_sem.at[k], device_id=pair, device_id_type=MESH)

    def to_cross(k):
        return pltpu.make_async_remote_copy(
            ys.at[k], yr.at[k], ys_sem.at[k], yr_sem.at[k], device_id=cross, device_id_type=MESH)

    for k in range(chunks + 1):
        if k < chunks:
            for copy in load(k):
                copy.wait()
            ps[k, 1] = delta(k, oy * 2 + oc)
            ps[k, 0] = delta(k, y * 2 + oc)
            to_pair(k).start()
        if k > 0:
            j = k - 1
            to_pair(j).wait_recv()
            ys[j] = (delta(j, oy * 2 + c).astype(jnp.float32) + pr[j, 1].astype(jnp.float32)).astype(jnp.bfloat16)
            to_cross(j).start()

    def send(yl, o, k, peer, sem):
        block = w.at[c, yl, o, k]
        return pltpu.make_async_remote_copy(
            block, block, sem, w_recv.at[c, yl, o, k], device_id=peer, device_id_type=MESH)

    def send_right(yl, o, k):
        return send(yl, o, k, right, right_sem.at[yl, o, k])

    def send_left(yl, o, k):
        return send(yl, o, k, left, left_sem.at[yl, o, k])

    def send_cross(yl, o, k):
        return send(yl, o, k, cross, cross_sem.at[o, k])

    def send_pair(yl, o, k):
        return send(yl, o, k, pair, pair_sem.at[yl, o, k])

    def arrived(cc, yl, o, k):
        block = w.at[cc, yl, o, k]
        pltpu.make_async_copy(block, block, w_recv.at[cc, yl, o, k]).wait()

    def along(yl, o, k, do_right, do_left):
        if do_right:
            @pl.when(z < depth - 1)
            def _():
                send_right(yl, o, k).start()
        if do_left:
            @pl.when(z > 0)
            def _():
                send_left(yl, o, k).start()

    def multiply(cc, yl, o, k):
        m, h, v = part(k)
        first = pl.multiple_of(((o * 4 + yl * 2 + cc) * HALVES + h) * rows, rows)
        acc[m, v] += jnp.dot(tok[:, pl.ds(first, rows)], w[cc, yl, o, k], preferred_element_type=jnp.float32)

    def normalize(i):
        at = pl.ds(pl.multiple_of(i * 16, 16), 16)
        value = tok[at, :].astype(jnp.float32)
        scale = lax.rsqrt(jnp.mean(value * value, axis=-1, keepdims=True) + epsilon)
        tok[at, :] = (value * scale * gain_ref[...]).astype(jnp.bfloat16)

    def out_copies(k):
        m, h, v = part(k)
        return (
            pltpu.make_async_copy(nb.at[k], nb_h.at[m, h, :, strip(v)], out_sem.at[k, 0]),
            pltpu.make_async_copy(mom.at[k], nm_h.at[m, h, :, strip(v)], out_sem.at[k, 1]),
        )

    load_tokens.wait()
    strips = token_rows // 16
    for k in range(chunks):
        lax.fori_loop(k * strips // chunks, (k + 1) * strips // chunks, lambda i, s: (normalize(i), s)[1], 0)
        load_momentum(k).wait()
        to_cross(k).wait_recv()
        total = (
            delta(k, r).astype(jnp.float32) + pr[k, 0].astype(jnp.float32) + yr[k].astype(jnp.float32))
        average = total / 4
        new_momentum = momentum_rate * mom[k] + average
        new_base = base[k, r] - outer_rate * (average + momentum_rate * new_momentum)
        w[c, y, z, k] = new_base.astype(jnp.bfloat16)
        mom[k] = new_momentum
        nb[k] = new_base
        along(y, z, k, True, True)
        send_cross(y, z, k).start()
        send_pair(y, z, k).start()
        for copy in out_copies(k):
            copy.start()

    def loop(count, body):
        lax.fori_loop(0, count, lambda i, s: (body(i), s)[1], 0)

    def both_sides(g, body):
        @pl.when(z - g >= 0)
        def _():
            body(z - g, True, False)

        @pl.when(z + g < depth)
        def _():
            body(z + g, False, True)

    def multiply_all(g, blocks, place):
        def one(i):
            cc, side, b = (i // 2) % 2, i % 2, i // 4
            o = z + (2 * side - 1) * g
            yl, k = place(b)

            @pl.when((o >= 0) & (o < depth))
            def _():
                @pl.when(cc == 1)
                def _():
                    arrived(oc, yl, o, k)
                multiply((c + cc) % 2, yl, o, k)
        loop(4 * blocks, one)

    def own_products(i):
        k, cc = i // 2, i % 2

        @pl.when(cc == 1)
        def _():
            arrived(oc, y, z, k)
        multiply((c + cc) % 2, y, z, k)

    loop(2 * chunks, own_products)

    late = chunks - first_z

    def first_stage(g):
        def one(k):
            def relay(o, do_right, do_left):
                arrived(c, y, o, k)
                along(y, o, k, do_right, do_left)
                send_cross(y, o, k).start()
                send_pair(y, o, k).start()
            both_sides(g, relay)
        loop(first_z, one)

        @pl.when(g == min(2, depth - 1))
        def _():
            for k in range(first_z, chunks):
                arrived(c, oy, z, k)
                along(oy, z, k, True, True)
                send_pair(oy, z, k).start()

        multiply_all(g, first_z, lambda b: (y, b))

    lax.fori_loop(1, depth, lambda g, s: (first_stage(g), s)[1], 0)

    def from_cross(k):
        arrived(c, oy, z, k)
        send_pair(oy, z, k).start()

    loop(first_z, from_cross)

    def cross_products(i):
        k, cc = i // 2, i % 2

        @pl.when(cc == 1)
        def _():
            arrived(oc, oy, z, k)
        multiply((c + cc) % 2, oy, z, k)

    loop(2 * chunks, cross_products)

    def second_stage(g):
        def one(i):
            yl, k = i % 2, first_z + i // 2

            def relay(o, do_right, do_left):
                arrived(c, yl, o, k)
                along(yl, o, k, do_right, do_left)
                send_pair(yl, o, k).start()
            both_sides(g, relay)
        loop(2 * late, one)
        multiply_all(g, 2 * late, lambda b: (b % 2, first_z + b // 2))

        def two(k):
            def relay(o, do_right, do_left):
                arrived(c, oy, o, k)
                send_pair(oy, o, k).start()
            both_sides(g, relay)
        loop(first_z, two)
        multiply_all(g, first_z, lambda b: (oy, b))

    lax.fori_loop(1, depth, lambda g, s: (second_stage(g), s)[1], 0)

    for v in range(strips_across):
        keys_ref[:, strip(v)] = acc[0, v].astype(keys_ref.dtype)
        values_ref[:, strip(v)] = acc[1, v].astype(values_ref.dtype)

    for k in range(chunks):
        to_pair(k).wait_send()
        to_cross(k).wait_send()
        for copy in out_copies(k):
            copy.wait()

    def drain(i):
        o, k = i // chunks, i % chunks

        @pl.when((k < first_z) | (o == z))
        def _():
            send_cross(y, o, k).wait_send()

        for yl in range(2):
            send_pair(yl, o, k).wait_send()

            @pl.when((k >= first_z) | (yl == y))
            def _():
                @pl.when((o <= z) & (z < depth - 1))
                def _():
                    send_right(yl, o, k).wait_send()

                @pl.when((o >= z) & (z > 0))
                def _():
                    send_left(yl, o, k).wait_send()

    loop(depth * chunks, drain)


def on_device(tokens, norm_gain, outer_base, momentum, inner_params):
    depth = lax.axis_size("fsdp")
    replicas = lax.axis_size("replica")
    assert replicas == 4
    quarter = outer_base.shape[1] // replicas
    rows, columns = quarter // HALVES, outer_base.shape[2]
    width = WIDTH if columns % WIDTH == 0 else columns
    chunks = 2 * HALVES * (columns // width)
    count, features = tokens.shape
    split = (2, replicas, HALVES, rows, columns)
    anywhere = pl.BlockSpec(memory_space=pl.ANY)
    vmem = pl.BlockSpec(memory_space=pltpu.VMEM)
    dma = pltpu.SemaphoreType.DMA
    f32, bf16 = jnp.float32, jnp.bfloat16
    piece, half = (rows, width), (rows, columns)
    new_base, new_momentum, keys, values = pl.pallas_call(
        functools.partial(kernel, depth, chunks),
        name="outer_step",
        out_shape=(
            jax.ShapeDtypeStruct((2, HALVES) + half, f32),
            jax.ShapeDtypeStruct((2, HALVES) + half, f32),
            jax.ShapeDtypeStruct((count, columns), bf16),
            jax.ShapeDtypeStruct((count, columns), bf16),
        ),
        in_specs=[anywhere, vmem, anywhere, anywhere, anywhere],
        out_specs=(anywhere, anywhere, vmem, vmem),
        scratch_shapes=[
            pltpu.VMEM((count, features), bf16),
            pltpu.VMEM((chunks, replicas) + piece, f32),
            pltpu.VMEM((chunks, replicas) + piece, bf16),
            pltpu.VMEM((chunks,) + piece, f32),
            pltpu.VMEM((chunks,) + piece, f32),
            pltpu.VMEM((2, 2, depth, chunks) + piece, bf16),
            pltpu.VMEM((chunks, 2) + piece, bf16),
            pltpu.VMEM((chunks, 2) + piece, bf16),
            pltpu.VMEM((chunks,) + piece, bf16),
            pltpu.VMEM((chunks,) + piece, bf16),
            pltpu.VMEM((2, columns // width, count, width), f32),
            dma((chunks, 3)), dma, dma((chunks, 2)),
            dma((chunks,)), dma((chunks,)), dma((chunks,)), dma((chunks,)),
            dma((2, 2, depth, chunks)),
            dma((2, depth, chunks)), dma((2, depth, chunks)), dma((depth, chunks)), dma((2, depth, chunks)),
        ],
        compiler_params=pltpu.CompilerParams(
            collective_id=0, has_side_effects=True, vmem_limit_bytes=60 * 1024 * 1024),
    )(
        tokens,
        norm_gain.reshape(1, features),
        outer_base.reshape(split),
        momentum.reshape(split),
        inner_params.reshape(split),
    )
    share = (2, quarter, columns)
    return new_base.reshape(share), new_momentum.reshape(share), keys, values


def solution(mesh):
    placed = (
        P(("replica", "fsdp"), None),
        P(),
        P(None, "fsdp", "tensor"),
        P(None, "fsdp", "tensor"),
        P("replica", None, "fsdp", "tensor"),
    )
    return jax.shard_map(
        on_device,
        mesh=mesh,
        in_specs=placed,
        out_specs=(
            P(None, ("fsdp", "replica"), "tensor"),
            P(None, ("fsdp", "replica"), "tensor"),
            P(("replica", "fsdp"), "tensor"),
            P(("replica", "fsdp"), "tensor"),
        ),
        check_vma=False,
    )
```

```python
import functools

import jax
import jax.numpy as jnp
from jax import lax
from jax.experimental import pallas as pl
from jax.experimental.pallas import tpu as pltpu
from jax.sharding import PartitionSpec as P

momentum_rate = 0.9
outer_rate = 0.7
epsilon = 1e-05
MESH = pl.DeviceIdType.MESH
CHUNKS = 4
FIRST_Z = 3


def kernel(
    depth, tok_h, gain_ref, base_h, mom_h, inner_h,
    nb_h, nm_h, keys_ref, values_ref,
    tok, base, inner, mom, nb, w, ps, pr, ys, yr, acc,
    in_sem, tok_sem, out_sem, ps_sem, pr_sem, ys_sem, yr_sem,
    w_recv, right_sem, left_sem, cross_sem, pair_sem,
):
    r = lax.axis_index("replica")
    z = lax.axis_index("fsdp")
    x = lax.axis_index("tensor")
    y, c = r // 2, r % 2
    oy, oc = 1 - y, 1 - c
    pair = (y * 2 + oc, z, x)
    cross = (oy * 2 + c, z, x)
    right = (r, z + 1, x)
    left = (r, z - 1, x)
    rows = w.shape[-2]
    token_rows = tok.shape[0]

    def load(k):
        m, h = k // 2, k % 2
        return (
            pltpu.make_async_copy(base_h.at[m, :, h], base.at[k], in_sem.at[k, 0]),
            pltpu.make_async_copy(inner_h.at[m, :, h], inner.at[k], in_sem.at[k, 1]),
        )

    def load_momentum(k):
        return pltpu.make_async_copy(mom_h.at[k // 2, r, k % 2], mom.at[k], in_sem.at[k, 2])

    load_tokens = pltpu.make_async_copy(tok_h, tok, tok_sem)
    for k in range(CHUNKS):
        for copy in load(k):
            copy.start()
    load_tokens.start()
    for k in range(CHUNKS):
        load_momentum(k).start()
    acc[...] = jnp.zeros_like(acc)

    barrier = pltpu.get_barrier_semaphore()
    for peer in (pair, cross):
        pl.semaphore_signal(barrier, inc=1, device_id=peer, device_id_type=MESH)

    @pl.when(z < depth - 1)
    def _():
        pl.semaphore_signal(barrier, inc=1, device_id=right, device_id_type=MESH)

    @pl.when(z > 0)
    def _():
        pl.semaphore_signal(barrier, inc=1, device_id=left, device_id_type=MESH)

    neighbours = jnp.where(z < depth - 1, 1, 0) + jnp.where(z > 0, 1, 0)
    pl.semaphore_wait(barrier, 2 + neighbours)

    def delta(k, target):
        return (base[k, target] - inner[k, target].astype(jnp.float32)).astype(jnp.bfloat16)

    def to_pair(k):
        return pltpu.make_async_remote_copy(
            ps.at[k], pr.at[k], ps_sem.at[k], pr_sem.at[k], device_id=pair, device_id_type=MESH)

    def to_cross(k):
        return pltpu.make_async_remote_copy(
            ys.at[k], yr.at[k], ys_sem.at[k], yr_sem.at[k], device_id=cross, device_id_type=MESH)

    for k in range(CHUNKS + 1):
        if k < CHUNKS:
            for copy in load(k):
                copy.wait()
            ps[k, 1] = delta(k, oy * 2 + oc)
            ps[k, 0] = delta(k, y * 2 + oc)
            to_pair(k).start()
        if k > 0:
            j = k - 1
            to_pair(j).wait_recv()
            ys[j] = (delta(j, oy * 2 + c).astype(jnp.float32) + pr[j, 1].astype(jnp.float32)).astype(jnp.bfloat16)
            to_cross(j).start()

    def send(yl, o, k, peer, sem):
        block = w.at[c, yl, o, k]
        return pltpu.make_async_remote_copy(
            block, block, sem, w_recv.at[c, yl, o, k], device_id=peer, device_id_type=MESH)

    def send_right(yl, o, k):
        return send(yl, o, k, right, right_sem.at[yl, o, k])

    def send_left(yl, o, k):
        return send(yl, o, k, left, left_sem.at[yl, o, k])

    def send_cross(yl, o, k):
        return send(yl, o, k, cross, cross_sem.at[o, k])

    def send_pair(yl, o, k):
        return send(yl, o, k, pair, pair_sem.at[yl, o, k])

    def arrived(cc, yl, o, k):
        block = w.at[cc, yl, o, k]
        pltpu.make_async_copy(block, block, w_recv.at[cc, yl, o, k]).wait()

    def along(yl, o, k, do_right, do_left):
        if do_right:
            @pl.when(z < depth - 1)
            def _():
                send_right(yl, o, k).start()
        if do_left:
            @pl.when(z > 0)
            def _():
                send_left(yl, o, k).start()

    def multiply(cc, yl, o, k):
        m, h = k // 2, k % 2
        first = pl.multiple_of(((o * 4 + yl * 2 + cc) * 2 + h) * rows, rows)
        acc[m] += jnp.dot(tok[:, pl.ds(first, rows)], w[cc, yl, o, k], preferred_element_type=jnp.float32)

    def normalize(i):
        at = pl.ds(pl.multiple_of(i * 16, 16), 16)
        value = tok[at, :].astype(jnp.float32)
        scale = lax.rsqrt(jnp.mean(value * value, axis=-1, keepdims=True) + epsilon)
        tok[at, :] = (value * scale * gain_ref[...]).astype(jnp.bfloat16)

    def out_copies(k):
        m, h = k // 2, k % 2
        return (
            pltpu.make_async_copy(nb.at[k], nb_h.at[m, h], out_sem.at[k, 0]),
            pltpu.make_async_copy(mom.at[k], nm_h.at[m, h], out_sem.at[k, 1]),
        )

    load_tokens.wait()
    strips = token_rows // 16
    for k in range(CHUNKS):
        lax.fori_loop(k * strips // CHUNKS, (k + 1) * strips // CHUNKS, lambda i, s: (normalize(i), s)[1], 0)
        load_momentum(k).wait()
        to_cross(k).wait_recv()
        total = (
            delta(k, r).astype(jnp.float32) + pr[k, 0].astype(jnp.float32) + yr[k].astype(jnp.float32))
        average = total / 4
        new_momentum = momentum_rate * mom[k] + average
        new_base = base[k, r] - outer_rate * (average + momentum_rate * new_momentum)
        w[c, y, z, k] = new_base.astype(jnp.bfloat16)
        mom[k] = new_momentum
        nb[k] = new_base
        along(y, z, k, True, True)
        send_cross(y, z, k).start()
        send_pair(y, z, k).start()
        for copy in out_copies(k):
            copy.start()

    def loop(count, body):
        lax.fori_loop(0, count, lambda i, s: (body(i), s)[1], 0)

    def both_sides(g, body):
        @pl.when(z - g >= 0)
        def _():
            body(z - g, True, False)

        @pl.when(z + g < depth)
        def _():
            body(z + g, False, True)

    def multiply_all(g, blocks, place):
        def one(i):
            cc, side, b = (i // 2) % 2, i % 2, i // 4
            o = z + (2 * side - 1) * g
            yl, k = place(b)

            @pl.when((o >= 0) & (o < depth))
            def _():
                @pl.when(cc == 1)
                def _():
                    arrived(oc, yl, o, k)
                multiply((c + cc) % 2, yl, o, k)
        loop(4 * blocks, one)

    def own_products(i):
        k, cc = i // 2, i % 2

        @pl.when(cc == 1)
        def _():
            arrived(oc, y, z, k)
        multiply((c + cc) % 2, y, z, k)

    loop(2 * CHUNKS, own_products)

    late = CHUNKS - FIRST_Z

    def first_stage(g):
        def one(k):
            def relay(o, do_right, do_left):
                arrived(c, y, o, k)
                along(y, o, k, do_right, do_left)
                send_cross(y, o, k).start()
                send_pair(y, o, k).start()
            both_sides(g, relay)
        loop(FIRST_Z, one)

        @pl.when(g == min(2, depth - 1))
        def _():
            for k in range(FIRST_Z, CHUNKS):
                arrived(c, oy, z, k)
                along(oy, z, k, True, True)
                send_pair(oy, z, k).start()

        multiply_all(g, FIRST_Z, lambda b: (y, b))

    lax.fori_loop(1, depth, lambda g, s: (first_stage(g), s)[1], 0)

    def from_cross(k):
        arrived(c, oy, z, k)
        send_pair(oy, z, k).start()

    loop(FIRST_Z, from_cross)

    def cross_products(i):
        k, cc = i // 2, i % 2

        @pl.when(cc == 1)
        def _():
            arrived(oc, oy, z, k)
        multiply((c + cc) % 2, oy, z, k)

    loop(2 * CHUNKS, cross_products)

    def second_stage(g):
        def one(i):
            yl, k = i % 2, FIRST_Z + i // 2

            def relay(o, do_right, do_left):
                arrived(c, yl, o, k)
                along(yl, o, k, do_right, do_left)
                send_pair(yl, o, k).start()
            both_sides(g, relay)
        loop(2 * late, one)
        multiply_all(g, 2 * late, lambda b: (b % 2, FIRST_Z + b // 2))

        def product(cc, k):
            def one_side(o, *_):
                @pl.when(cc == oc)
                def _():
                    arrived(oc, oy, o, k)
                multiply(cc, oy, o, k)
            both_sides(g, one_side)

        def two(k):
            def relay(o, do_right, do_left):
                arrived(c, oy, o, k)
                send_pair(oy, o, k).start()
            both_sides(g, relay)
            product(c, k)

            @pl.when(k > 0)
            def _():
                product(oc, k - 1)
        loop(FIRST_Z, two)
        product(oc, FIRST_Z - 1)

    lax.fori_loop(1, depth, lambda g, s: (second_stage(g), s)[1], 0)

    keys_ref[...] = acc[0].astype(keys_ref.dtype)
    values_ref[...] = acc[1].astype(values_ref.dtype)

    for k in range(CHUNKS):
        to_pair(k).wait_send()
        to_cross(k).wait_send()
        for copy in out_copies(k):
            copy.wait()

    def drain(i):
        o, k = i // CHUNKS, i % CHUNKS

        @pl.when((k < FIRST_Z) | (o == z))
        def _():
            send_cross(y, o, k).wait_send()

        for yl in range(2):
            send_pair(yl, o, k).wait_send()

            @pl.when((k >= FIRST_Z) | (yl == y))
            def _():
                @pl.when((o <= z) & (z < depth - 1))
                def _():
                    send_right(yl, o, k).wait_send()

                @pl.when((o >= z) & (z > 0))
                def _():
                    send_left(yl, o, k).wait_send()

    loop(depth * CHUNKS, drain)


def on_device(tokens, norm_gain, outer_base, momentum, inner_params):
    depth = lax.axis_size("fsdp")
    replicas = lax.axis_size("replica")
    assert replicas == 4
    quarter = outer_base.shape[1] // replicas
    rows, columns = quarter // 2, outer_base.shape[2]
    count, features = tokens.shape
    split = (2, replicas, 2, rows, columns)
    anywhere = pl.BlockSpec(memory_space=pl.ANY)
    vmem = pl.BlockSpec(memory_space=pltpu.VMEM)
    dma = pltpu.SemaphoreType.DMA
    f32, bf16 = jnp.float32, jnp.bfloat16
    piece = (rows, columns)
    new_base, new_momentum, keys, values = pl.pallas_call(
        functools.partial(kernel, depth),
        name="outer_step",
        out_shape=(
            jax.ShapeDtypeStruct((2, 2) + piece, f32),
            jax.ShapeDtypeStruct((2, 2) + piece, f32),
            jax.ShapeDtypeStruct((count, columns), bf16),
            jax.ShapeDtypeStruct((count, columns), bf16),
        ),
        in_specs=[anywhere, vmem, anywhere, anywhere, anywhere],
        out_specs=(anywhere, anywhere, vmem, vmem),
        scratch_shapes=[
            pltpu.VMEM((count, features), bf16),
            pltpu.VMEM((CHUNKS, replicas) + piece, f32),
            pltpu.VMEM((CHUNKS, replicas) + piece, bf16),
            pltpu.VMEM((CHUNKS,) + piece, f32),
            pltpu.VMEM((CHUNKS,) + piece, f32),
            pltpu.VMEM((2, 2, depth, CHUNKS) + piece, bf16),
            pltpu.VMEM((CHUNKS, 2) + piece, bf16),
            pltpu.VMEM((CHUNKS, 2) + piece, bf16),
            pltpu.VMEM((CHUNKS,) + piece, bf16),
            pltpu.VMEM((CHUNKS,) + piece, bf16),
            pltpu.VMEM((2, count, columns), f32),
            dma((CHUNKS, 3)), dma, dma((CHUNKS, 2)),
            dma((CHUNKS,)), dma((CHUNKS,)), dma((CHUNKS,)), dma((CHUNKS,)),
            dma((2, 2, depth, CHUNKS)),
            dma((2, depth, CHUNKS)), dma((2, depth, CHUNKS)), dma((depth, CHUNKS)), dma((2, depth, CHUNKS)),
        ],
        compiler_params=pltpu.CompilerParams(
            collective_id=0, has_side_effects=True, vmem_limit_bytes=60 * 1024 * 1024),
    )(
        tokens,
        norm_gain.reshape(1, features),
        outer_base.reshape(split),
        momentum.reshape(split),
        inner_params.reshape(split),
    )
    share = (2, quarter, columns)
    return new_base.reshape(share), new_momentum.reshape(share), keys, values


def solution(mesh):
    placed = (
        P(("replica", "fsdp"), None),
        P(),
        P(None, "fsdp", "tensor"),
        P(None, "fsdp", "tensor"),
        P("replica", None, "fsdp", "tensor"),
    )
    return jax.shard_map(
        on_device,
        mesh=mesh,
        in_specs=placed,
        out_specs=(
            P(None, ("fsdp", "replica"), "tensor"),
            P(None, ("fsdp", "replica"), "tensor"),
            P(("replica", "fsdp"), "tensor"),
            P(("replica", "fsdp"), "tensor"),
        ),
        check_vma=False,
    )
```
